32 devices in a mesh: dp: 16 (over z, y, x), mp: 2 (over core).
Axes of the slice: x: 2, y: 2, z: 4, core: 2. Of those that a mesh axis runs over, the one named last changes fastest.
Arguments:
- gradients: float32 [16, 4, 32, 8192], P('dp', None, 'mp'), may hold values from -6 to 6
- weights: float32 [4, 32, 8192], P(None, 'mp', 'dp'), may hold values from -40 to 40
- first_moment: float32 [4, 32, 8192], P(None, 'mp', 'dp'), may hold values from -0.6 to 0.6
- second_moment: float32 [4, 32, 8192], P(None, 'mp', 'dp'), may hold values from 0.001 to 0.1
- learn_rate: float32 [4], replicated, may hold values from 0.1 to 0.5
- weight_decay: float32 [4], replicated, may hold values from 0.1 to 1
Outputs:
- new_weights: float32 [4, 32, 8192], P(None, 'mp')
- new_first: float32 [4, 32, 8192], P(None, 'mp', 'dp')
- new_second: float32 [4, 32, 8192], P(None, 'mp', 'dp')
- trust_ratio: float32 [4], replicated
The draws below stay inside these ranges and needn't reach their ends.
All inputs are finite; a program needn't handle non-finite values.
Results may differ from the reference program's by a relative error of at most 0.000062.
Values sent between devices are 32-bit elements; how exact they have to be, the bound alone decides.
No kernel may reach another device: no remote copies, remote signals or barrier semaphores. Data moves between devices by JAX's collectives and lax.ppermute only.
A program may use at most 64 MiB of HBM per device.

```python
import math
import jax
import jax.numpy as jnp
from jax import lax

D = 8192
NT = 4
STEP = 10
ROWS = 32
REPLICAS = 16
N_DP = 16


def draw_weights(key, part):
    base_key = jax.random.fold_in(key, 11)
    row_key = jax.random.fold_in(key, 12)
    col_key = jax.random.fold_in(key, 13)
    row_place = jnp.arange(ROWS, dtype=jnp.float32) / ROWS
    col_place = jnp.arange(D, dtype=jnp.float32) / D
    row_scale = jnp.exp(math.log(3.0) * row_place + jax.random.uniform(row_key, (ROWS,), jnp.float32, 0.0, math.log(3.3)))
    col_scale = jnp.exp(math.log(3.0) * col_place + jax.random.uniform(col_key, (D,), jnp.float32, 0.0, math.log(3.3)))
    base = jax.random.truncated_normal(base_key, -4.0, 4.0, (NT, ROWS, D), jnp.float32)
    return 0.1 * base * row_scale[None, :, None] * col_scale[None, None, :]


def spiked(array, key, source, target, shards_of, factor):
    def block_of(position):
        return (jnp.arange(array.shape[position]) // (array.shape[position] // shards_of)).reshape((-1,) + (1,) * (array.ndim - 1 - position))

    one_side = jax.random.permutation(key, shards_of)[block_of(target)]
    far = (block_of(target) + shards_of // 2) % shards_of
    return jnp.where((block_of(source) == one_side) | (block_of(source) == far), factor * array, array)


def block_levels(rng, dims, cuts, least, top_value):
    gain = 1.0
    for position, shards_of in cuts:
        draws = jax.random.uniform(jax.random.fold_in(jax.random.fold_in(rng, 6), position), (shards_of,), jnp.float32, least / len(cuts), top_value / len(cuts))
        gain = gain * jnp.repeat(jnp.exp(draws), dims[position] // shards_of).reshape((-1,) + (1,) * (len(dims) - 1 - position))
    return gain


def centred(rng, extent, width, bound, split=(), held_as=jnp.bfloat16):
    drawn = width * jax.random.normal(rng, extent, jnp.float32)
    if split:
        drawn = drawn * block_levels(rng, extent, split, -0.22, 0.18)
    return jnp.clip(drawn, -bound, bound).astype(held_as)


def heavy_noise(key, shape, scale, bound, cuts, heavy, kind=jnp.bfloat16):
    result = scale * jax.random.normal(key, shape, jnp.float32)
    if cuts:
        result = result * block_levels(key, shape, cuts, -0.22, 0.18)
    return jnp.clip(spiked(result, jax.random.fold_in(key, 3), *heavy), -bound, bound).astype(kind)


def setup_inputs(seed: int = 0) -> dict:
    key_list = jax.random.split(jax.random.key(seed), 7)
    gradients = heavy_noise(key_list[0], (REPLICAS, NT, ROWS, D), 1.0, 6.0, ((0, 16), (2, 2)), (0, 3, 16, 2.0), jnp.float32)
    weights = draw_weights(jax.random.fold_in(key_list[6], 71), 0)
    first_moment = centred(key_list[2], (NT, ROWS, D), 0.1, 0.6, ((1, 2), (2, 16)), jnp.float32)
    second_moment = jnp.clip(jnp.exp(math.log(0.1) - 4.6051702 * jax.random.uniform(key_list[3], (NT, ROWS, D), jnp.float32) ** block_levels(key_list[3], (NT, ROWS, D), ((1, 2), (2, 16)), -0.2, 0.2)), 0.001, 0.1)
    learn_rate = jnp.clip(jnp.exp(jax.random.uniform(key_list[4], (NT,), jnp.float32, math.log(0.1), math.log(0.5))), 0.1, 0.5)
    weight_decay = jnp.clip(jax.random.uniform(key_list[5], (NT,), jnp.float32, 0.1, 1.0), 0.1, 1.0)
    return {"gradients": gradients, "weights": weights, "first_moment": first_moment, "second_moment": second_moment, "learn_rate": learn_rate, "weight_decay": weight_decay}


def reference(gradients, weights, first_moment, second_moment, learn_rate, weight_decay):
    summed = lax.optimization_barrier(jnp.sum(gradients, axis=0)) * (1.0 / N_DP)
    new_first = 0.9 * first_moment + 0.1 * summed
    new_second = 0.999 * second_moment + 0.001 * summed * summed
    first_fix = 1.0 - 0.9 ** STEP
    second_fix = 1.0 - 0.999 ** STEP
    update = new_first / first_fix / (jnp.sqrt(new_second / second_fix) + 1e-06) + weight_decay[:, None, None] * weights
    weight_sq = lax.optimization_barrier(jnp.sum(weights * weights, axis=(1, 2)))
    update_sq = lax.optimization_barrier(jnp.sum(update * update, axis=(1, 2)))
    trust_ratio = jnp.sqrt(weight_sq) / (jnp.sqrt(update_sq) + 1e-06)
    new_weights = weights - (learn_rate * trust_ratio)[:, None, None] * update
    return (new_weights, new_first, new_second, trust_ratio)
```

```python
import jax
import jax.numpy as jnp
from jax import lax
from jax.sharding import PartitionSpec as P

STEP = 10
SUB, LANE = 8, 128


def tiles(a):
    t, r, c = a.shape
    a = a.reshape(t, r // SUB, SUB, c // LANE, LANE)
    return a.transpose(0, 1, 3, 2, 4).reshape(t * (r // SUB), c // LANE, SUB, LANE)


def untiles(a, t, r):
    c = a.shape[1]
    a = a.reshape(t, r // SUB, c, SUB, LANE).transpose(0, 1, 3, 2, 4)
    return a.reshape(t, r, c * LANE)


def swap(a, axis, bit):
    n = lax.axis_size(axis)
    return lax.ppermute(a, axis, [(i, i ^ (1 << bit)) for i in range(n)])


def pick(a, k):
    return lax.dynamic_index_in_dim(a, k, 1, keepdims=False)


class Block:
    def __init__(self, addends, left):
        self.addends, self.left = addends, left

    def halves(self, bit, b):
        at = self.left.index(bit)
        send, keep = [], []
        for a in self.addends:
            send.append(lax.dynamic_index_in_dim(a, 1 - b, 1 + at, keepdims=False))
            keep.append(lax.dynamic_index_in_dim(a, b, 1 + at, keepdims=False))
        left = tuple(x for x in self.left if x != bit)
        return sum(send[1:], send[0]), Block(keep, left)


def shards(gradients, weights, first_moment, second_moment, learn_rate, weight_decay):
    n = lax.axis_size("dp")
    bits = n.bit_length() - 1
    me = lax.axis_index("dp")
    b = [(me >> i) & 1 for i in range(bits)]
    nt, rows, _ = weights.shape
    g = tiles(gradients[0])
    high = tuple(reversed(range(bits)))
    g = g.reshape((g.shape[0],) + (2,) * bits + (g.shape[1] // n, SUB, LANE))
    half = g.shape[0] // 2
    pair = [Block([g[:half]], high), Block([g[half:]], high)]
    orders = [(0, 1), (1, 0)]
    for phase in range(2):
        for s in range(2):
            bit = orders[s][phase]
            send, pair[s] = pair[s].halves(bit, b[bit])
            pair[s].addends.append(swap(send, "dp", bit))
    whole = Block([jnp.concatenate([sum(p.addends[1:], p.addends[0]) for p in pair])], pair[0].left)
    for bit in range(2, bits):
        send, whole = whole.halves(bit, b[bit])
        whole.addends.append(swap(send, "dp", bit))
    summed = sum(whole.addends[1:], whole.addends[0]) * (1.0 / n)

    w, m, v = tiles(weights), tiles(first_moment), tiles(second_moment)
    per = w.shape[0] // nt
    new_first = 0.9 * m + 0.1 * summed
    new_second = 0.999 * v + 0.001 * summed * summed
    first_fix = 1.0 - 0.9**STEP
    second_fix = 1.0 - 0.999**STEP
    decay = jnp.repeat(weight_decay, per)[:, None, None, None]
    update = new_first / first_fix / (jnp.sqrt(new_second / second_fix) + 1e-06) + decay * w

    def squares(a):
        return jnp.sum((a * a).reshape(nt, -1), axis=1)

    sq = jnp.stack([squares(w), squares(update)])
    for axis in ("mp", "dp"):
        for bit in range(lax.axis_size(axis).bit_length() - 1):
            sq = sq + swap(sq, axis, bit)
    trust_ratio = jnp.sqrt(sq[0]) / (jnp.sqrt(sq[1]) + 1e-06)
    rate = jnp.repeat(learn_rate * trust_ratio, per)[:, None, None, None]
    full = w - rate * update

    def joined(a, bit, at):
        other = swap(a, "dp", bit)
        low, high = jnp.where(b[bit] == 0, a, other), jnp.where(b[bit] == 0, other, a)
        return jnp.stack([low, high], axis=at)

    for bit in reversed(range(2, bits)):
        full = joined(full, bit, 1 + bits - 1 - bit)
    pair = [full[:half], full[half:]]
    for phase in reversed(range(2)):
        pair = [joined(pair[s], orders[s][phase], bits - 1 + (1 - phase if s == 0 else 0)) for s in range(2)]
    full = jnp.concatenate(pair)
    full = full.reshape(full.shape[0], -1, SUB, LANE)
    return (
        untiles(full, nt, rows),
        untiles(new_first, nt, rows),
        untiles(new_second, nt, rows),
        trust_ratio,
    )


def solution(mesh):
    in_specs = (
        P("dp", None, "mp", None),
        P(None, "mp", "dp"),
        P(None, "mp", "dp"),
        P(None, "mp", "dp"),
        P(),
        P(),
    )
    out_specs = (P(None, "mp", None), P(None, "mp", "dp"), P(None, "mp", "dp"), P())
    return jax.shard_map(shards, mesh=mesh, in_specs=in_specs, out_specs=out_specs, check_vma=False)
```

```python
import jax
import jax.numpy as jnp
from jax import lax
from jax.sharding import PartitionSpec as P


STEP = 10
SUB, LANE = 8, 128


def tiles(a):
    t, r, c = a.shape
    a = a.reshape(t, r // SUB, SUB, c // LANE, LANE)
    return a.transpose(0, 1, 3, 2, 4).reshape(t * (r // SUB), c // LANE, SUB, LANE)


def untiles(a, t, r):
    c = a.shape[1]
    a = a.reshape(t, r // SUB, c, SUB, LANE).transpose(0, 1, 3, 2, 4)
    return a.reshape(t, r, c * LANE)


def swap(a, axis, bit):
    n = lax.axis_size(axis)
    return lax.ppermute(a, axis, [(i, i ^ (1 << bit)) for i in range(n)])


class Part:
    def __init__(self, array, low, dims, chosen=()):
        self.array, self.low, self.dims, self.chosen = array, low, dims, dict(chosen)

    def at(self, bit, value):
        return Part(self.array, self.low, self.dims, {**self.chosen, bit: value})

    def read(self, rows):
        block = self.array.shape[1 + len(self.dims) :]
        zero = jnp.uint32(0)
        first = [jnp.uint32(self.low)] + [self.chosen.get(d, zero) for d in self.dims] + [zero] * len(block)
        size = [rows] + [1 if d in self.chosen else 2 for d in self.dims] + list(block)
        left = [2 for d in self.dims if d not in self.chosen]
        return lax.dynamic_slice(self.array, first, size).reshape([rows] + left + list(block))


def total(parts, rows):
    out = parts[0].read(rows)
    for part in parts[1:]:
        out = out + part.read(rows)
    return out


def shards(gradients, weights, first_moment, second_moment, learn_rate, weight_decay):
    n = lax.axis_size("dp")
    bits = n.bit_length() - 1
    me = lax.axis_index("dp")
    b = [((me >> i) & 1).astype(jnp.uint32) for i in range(bits)]
    not_b = [1 - x for x in b]
    g, b, not_b = lax.optimization_barrier((gradients[0], b, not_b))
    nt, rows, _ = weights.shape
    g = tiles(g)
    every = tuple(reversed(range(bits)))
    g = g.reshape((g.shape[0],) + (2,) * bits + (g.shape[1] // n, SUB, LANE))
    half = g.shape[0] // 2
    low = [0, half]
    orders = [(0, 1) + tuple(range(2, bits)), (1, 0) + tuple(range(2, bits))]
    flat = g.reshape(g.shape[: 1 + bits] + (-1, LANE))
    streams = [[Part(g, low[0], every)], [Part(flat, low[1], every)]]
    left = [every, every]
    for phase in range(bits):
        for s in range(2):
            bit = orders[s][phase]
            send = total([p.at(bit, not_b[bit]) for p in streams[s]], half)
            got = swap(send, "dp", bit)
            streams[s] = [p.at(bit, b[bit]) for p in streams[s]]
            left[s] = tuple(d for d in left[s] if d != bit)
            streams[s].append(Part(got, 0, left[s]))
    summed = [(total(p, half) * (1.0 / n)).reshape((half,) + g.shape[-3:]) for p in streams]

    w, m, v = tiles(weights), tiles(first_moment), tiles(second_moment)
    first_fix = 1.0 - 0.9**STEP
    second_fix = 1.0 - 0.999**STEP
    each = nt // 2

    def scaled(factors, s, a):
        factors = factors[s * each : (s + 1) * each]
        return (a.reshape((each, -1) + a.shape[1:]) * factors.reshape((each,) + (1,) * a.ndim)).reshape(a.shape)

    new_first, new_second, update = [], [], []
    for s in range(2):
        own = slice(low[s], low[s] + half)
        first = 0.9 * m[own] + 0.1 * summed[s]
        second = 0.999 * v[own] + 0.001 * summed[s] * summed[s]
        new_first.append(first)
        new_second.append(second)
        step = first / first_fix / (jnp.sqrt(second / second_fix) + 1e-06)
        update.append(step + scaled(weight_decay, s, w[own]))
    new_first, new_second = jnp.concatenate(new_first), jnp.concatenate(new_second)
    update = jnp.concatenate(update)

    def squares(a):
        return jnp.sum((a * a).reshape(nt, -1), axis=1)

    update, sq = lax.optimization_barrier((update, jnp.stack([squares(w), squares(update)])))

    def joined(a, bit, at):
        other = swap(a, "dp", bit)
        low, high = jnp.where(b[bit] == 0, a, other), jnp.where(b[bit] == 0, other, a)
        return jnp.stack([low, high], axis=at)

    def widened(a):
        for bit in reversed(range(2, bits)):
            a = joined(a, bit, 1 + bits - 1 - bit)
        parts = [a[:half], a[half:].reshape((half,) + a.shape[1:-3] + (-1, LANE))]
        return [joined(parts[s], orders[s][1], bits - 1) for s in range(2)]

    wide_w, wide_u = widened(w), widened(update)
    for axis, order in (("mp", range(lax.axis_size("mp").bit_length() - 1)), ("dp", [0, 1] + list(reversed(range(2, bits))))):
        for bit in order:
            sq = sq + swap(sq, axis, bit)
    trust_ratio = jnp.sqrt(sq[0]) / (jnp.sqrt(sq[1]) + 1e-06)
    rate = learn_rate * trust_ratio
    full = [wide_w[s] - scaled(rate, s, wide_u[s]) for s in range(2)]
    full = [joined(full[s], orders[s][0], bits if s == 0 else bits - 1) for s in range(2)]
    full = jnp.concatenate([a.reshape(half, -1, SUB, LANE) for a in full])
    return (
        untiles(full, nt, rows),
        untiles(new_first, nt, rows),
        untiles(new_second, nt, rows),
        trust_ratio,
    )


def solution(mesh):
    in_specs = (
        P("dp", None, "mp", None),
        P(None, "mp", "dp"),
        P(None, "mp", "dp"),
        P(None, "mp", "dp"),
        P(),
        P(),
    )
    out_specs = (P(None, "mp", None), P(None, "mp", "dp"), P(None, "mp", "dp"), P())

    return jax.shard_map(shards, mesh=mesh, in_specs=in_specs, out_specs=out_specs, check_vma=False)
```
